32 devices in a mesh: shard: 4 (over x, core), rep: 8 (over z, y).
Axes of the slice: x: 2, y: 2, z: 4, core: 2. Of those that a mesh axis runs over, the one named last changes fastest.
Arguments:
- tokens: bfloat16 [16384, 512], P(('shard', 'rep')), may hold values from -6 to 6
- cotangent: bfloat16 [16384, 512], P(('shard', 'rep')), may hold values from -6 to 6
- segments: int32 [16384], P(('shard', 'rep')), may hold values from 0 to 7, as said below
- positions: int32 [16384], P(('shard', 'rep')), may hold values from 0 to 255, as said below
- params: float32 [3152384], P('shard')
- first_moment: float32 [3152384], P('shard'), may hold values from -0.6 to 0.6
- second_moment: float32 [3152384], P('shard'), may hold values from 0.02 to 0.2
Outputs:
- mixed: bfloat16 [16384, 512], P(('shard', 'rep'))
- input_grad: bfloat16 [16384, 512], P(('shard', 'rep'))
- param_grad: float32 [3152384], P('shard')
- param_update: float32 [3152384], P('shard')
- new_first: float32 [3152384], P('shard')
- new_second: float32 [3152384], P('shard')
The draws below stay inside these ranges and needn't reach their ends.
Inputs may be any that keep to these rules, and one draw needn't show every extreme that they name: `segments`: each sequence of 512 tokens holds exactly 8 documents, numbered 0 to 7 in order. `positions`: 0 at the first token of each document, rising by one along it; in each sequence one document has exactly 256 tokens, the others fewer.
All inputs are finite; a program needn't handle non-finite values.
Results may differ from the reference program's by a relative error of at most 0.012.
Values may be sent and summed in bfloat16 or wider, within the bound.
No kernel may reach another device: no remote copies, remote signals or barrier semaphores. Data moves between devices by JAX's collectives and lax.ppermute only.
A program may use at most 128 MiB of HBM per device.

```python
import math
import jax
import jax.numpy as jnp
from jax import lax

D = 512
HEADS = 8
HEAD = 64
ROT = 16
FF = 2048
TOK_DEV = 512
STEP = 4
TOKENS = 16384
P_SIZE = 3152384


def one_layout(key):
    half_len = TOK_DEV // 2
    shuffled = jax.random.permutation(jax.random.fold_in(key, 3), half_len - 1) + 1
    cut_points = jnp.sort(shuffled[:6]).astype(jnp.int32)
    short_starts = jnp.concatenate([jnp.zeros((1,), jnp.int32), cut_points, jnp.full((1,), half_len, jnp.int32)])
    long_place = jax.random.randint(jax.random.fold_in(key, 5), (), 0, 8)
    doc_index = jnp.arange(8, dtype=jnp.int32)
    before = short_starts[:8]
    after = short_starts[jnp.maximum(doc_index - 1, 0)] + half_len
    doc_starts = jnp.where(doc_index <= long_place, before, after).astype(jnp.int32)
    indices = jnp.arange(TOK_DEV, dtype=jnp.int32)
    reached = doc_starts[None, :] <= indices[:, None]
    seg_ids = jnp.sum(reached.astype(jnp.int32), axis=1) - 1
    start_of = jnp.max(jnp.where(reached, doc_starts[None, :], 0), axis=1)
    return (seg_ids.astype(jnp.int32), (indices - start_of).astype(jnp.int32))


def doc_layout(key):
    seq_count = TOKENS // TOK_DEV
    base = jax.random.fold_in(key, 7)
    seq_keys = jax.vmap(lambda number: jax.random.fold_in(base, number))(jnp.arange(seq_count, dtype=jnp.int32))
    seg_ids, places = jax.vmap(one_layout)(seq_keys)
    return (seg_ids.reshape(-1).astype(jnp.int32), places.reshape(-1).astype(jnp.int32))


def draw_segments(key, part):
    return doc_layout(key)[0]


def draw_positions(key, part):
    return doc_layout(key)[1]


def draw_params(key, part):
    subkeys = jax.random.split(key, 12)

    def sample(number, extent, spread):
        return spread * jax.random.normal(subkeys[number], extent, jnp.float32)
    pieces = [sample(0, (D, 3 * D), D ** (-0.5)), sample(1, (D, D), 4.0 * D ** (-0.5)), sample(2, (D, FF), D ** (-0.5)), sample(3, (FF, D), FF ** (-0.5)), sample(4, (3 * D,), 0.5), sample(5, (D,), 0.3), sample(6, (FF,), 0.5), sample(7, (D,), 0.3), 1.0 + sample(8, (D,), 0.2), sample(9, (D,), 0.2), 1.0 + sample(10, (D,), 0.2), sample(11, (D,), 0.2)]
    return jnp.concatenate([piece.reshape(-1) for piece in pieces]).astype(jnp.float32)


def level_of(stream_key, shape, cuts, smallest, top_value):
    gain, own = 1.0, jax.random.fold_in(stream_key, 6)
    for position, shards_of in cuts:
        heights = jnp.exp(jax.random.uniform(jax.random.fold_in(own, position), (shards_of,), jnp.float32, smallest / len(cuts), top_value / len(cuts)))
        gain = gain * jnp.repeat(heights, shape[position] // shards_of).reshape([-1 if axis == position else 1 for axis in range(len(shape))])
    return gain


def scatter_about(rng, dims, deviation, bound, shards=(), held_as=jnp.bfloat16):
    array = jax.random.normal(rng, dims, jnp.float32) * deviation
    if len(shards) > 0:
        array = level_of(rng, dims, shards, -0.22, 0.18) * array
    return jnp.clip(array, min=-bound, max=bound).astype(held_as)


def setup_inputs(seed: int = 0) -> dict:
    key_of = jax.random.split(jax.random.key(seed), 8)
    tokens = scatter_about(key_of[0], (TOKENS, D), 1.0, 6.0, ((0, 32),))
    cotangent = scatter_about(key_of[1], (TOKENS, D), 1.0, 6.0, ((0, 32),))
    segments = draw_segments(jax.random.fold_in(key_of[7], 71), 0)
    positions = draw_positions(jax.random.fold_in(key_of[7], 71), 0)
    params = draw_params(jax.random.fold_in(key_of[7], 71), 0)
    first_moment = scatter_about(key_of[5], (P_SIZE,), 0.1, 0.6, ((0, 4),), jnp.float32)
    second_moment = jnp.clip(jnp.exp(math.log(0.2) - 2.3025851 * jax.random.uniform(key_of[6], (P_SIZE,), jnp.float32) ** level_of(key_of[6], (P_SIZE,), ((0, 4),), -0.2, 0.2)), 0.02, 0.2)
    return {"tokens": tokens, "cotangent": cotangent, "segments": segments, "positions": positions, "params": params, "first_moment": first_moment, "second_moment": second_moment}


@jax.custom_vjp
def low(v):
    return lax.optimization_barrier(v.astype(jnp.bfloat16)).astype(jnp.float32)

@jax.custom_vjp
def low_back(v):
    return v

def low_keep(v):
    return (low(v), None)

def low_pass(kept, grad):
    return (grad,)

def back_keep(v):
    return (v, None)

def back_low(kept, grad):
    return (low(grad),)
low.defvjp(low_keep, low_pass)
low_back.defvjp(back_keep, back_low)
NEG_FILL = -1e+30
NORM_EPS = 1e-05
ROPE_BASE = 10000.0

def unflatten(flat_params):
    extents = [(D, 3 * D), (D, D), (D, FF), (FF, D), (3 * D,), (D,), (FF,), (D,), (D,), (D,), (D,), (D,)]
    pieces = []
    offset = 0
    for extent in extents:
        length = int(math.prod(extent))
        pieces.append(flat_params[offset:offset + length].reshape(extent))
        offset = offset + length
    return pieces

def rotary_tables(places):
    half_rot = ROT // 2
    frequency = ROPE_BASE ** (-jnp.arange(half_rot, dtype=jnp.float32) * 2.0 / ROT)
    angles = places.astype(jnp.float32)[:, None] * frequency[None, :]
    return (jnp.cos(angles)[:, None, :], jnp.sin(angles)[:, None, :])

def rotate(values_in, cos_table, sin_table):
    half_rot = ROT // 2
    first_half = values_in[..., :half_rot]
    second_half = values_in[..., half_rot:ROT]
    return jnp.concatenate([first_half * cos_table - second_half * sin_table, second_half * cos_table + first_half * sin_table, values_in[..., ROT:]], axis=-1)

def attention(queries, keys_all, values_all, segs):
    seq_len = queries.shape[1]
    block_rows = min(512, seq_len)
    columns = jnp.arange(seq_len, dtype=jnp.int32)

    def one_block(row_start):
        query_block = lax.dynamic_slice_in_dim(queries, row_start, block_rows, axis=1)
        scores = jnp.einsum('hqd,hkd->hqk', query_block, keys_all, precision=lax.Precision.HIGHEST) * HEAD ** (-0.5)
        row_ids = row_start + jnp.arange(block_rows, dtype=jnp.int32)
        row_segs = lax.dynamic_slice_in_dim(segs, row_start, block_rows)
        allowed = (columns[None, :] <= row_ids[:, None]) & (row_segs[:, None] == segs[None, :])
        scores = low_back(jnp.where(allowed[None], scores, NEG_FILL))
        row_peak = lax.optimization_barrier(jnp.max(scores, axis=-1, keepdims=True))
        exp_terms = jnp.exp(scores - row_peak)
        prob_low = low(exp_terms / lax.optimization_barrier(jnp.sum(exp_terms, axis=-1, keepdims=True)))
        return jnp.einsum('hqk,hkd->hqd', prob_low, values_all, precision=lax.Precision.HIGHEST)
    starts = jnp.arange(seq_len // block_rows, dtype=jnp.int32) * block_rows
    blocks = lax.map(jax.checkpoint(one_block), starts)
    return blocks.transpose(1, 0, 2, 3).reshape(HEADS, seq_len, HEAD)

def layer(layer_in, flat_params, segs, places):
    w_qkv, w_out, w_up, w_down, b_qkv, b_out, b_up, b_down, gain_one, shift_one, gain_two, shift_two = unflatten(low(flat_params))
    seq_len = layer_in.shape[0]
    center = layer_in - lax.optimization_barrier(jnp.mean(layer_in, axis=1, keepdims=True))
    normed = center * lax.rsqrt(lax.optimization_barrier(jnp.mean(center * center, axis=1, keepdims=True)) + NORM_EPS)
    attn_in = low(normed * gain_one + shift_one)
    mlp_in = low(normed * gain_two + shift_two)
    projected = low_back(jnp.dot(attn_in, w_qkv, precision=lax.Precision.HIGHEST) + b_qkv)
    heads_view = projected.reshape(seq_len, 3, HEADS, HEAD)
    cos_table, sin_table = rotary_tables(places)
    queries = low(rotate(heads_view[:, 0], cos_table, sin_table)).transpose(1, 0, 2)
    keys_all = low(rotate(heads_view[:, 1], cos_table, sin_table)).transpose(1, 0, 2)
    values_all = low(heads_view[:, 2]).transpose(1, 0, 2)
    attended = attention(queries, keys_all, values_all, segs)
    merged = low_back(low(attended.transpose(1, 0, 2).reshape(seq_len, D)))
    attn_branch = jnp.dot(merged, w_out, precision=lax.Precision.HIGHEST) + b_out
    hidden = low_back(jnp.dot(mlp_in, w_up, precision=lax.Precision.HIGHEST) + b_up)
    activated = low(0.5 * hidden * (1.0 + jax.scipy.special.erf(hidden * (1.0 / math.sqrt(2.0)))))
    mlp_branch = jnp.dot(activated, w_down, precision=lax.Precision.HIGHEST) + b_down
    return layer_in + attn_branch + mlp_branch

def reference(tokens, cotangent, segments, positions, params, first_moment, second_moment):
    seq_count = TOKENS // TOK_DEV
    inputs = tokens.astype(jnp.float32).reshape(seq_count, TOK_DEV, D)
    upstream = cotangent.astype(jnp.float32).reshape(seq_count, TOK_DEV, D)
    seg_rows = segments.reshape(seq_count, TOK_DEV).astype(jnp.int32)
    place_rows = positions.reshape(seq_count, TOK_DEV).astype(jnp.int32)
    weights = params.astype(jnp.float32)

    def one_sequence(running, packed):
        seq_in, seq_cot, seq_segs, seq_places = packed
        output, pullback = jax.vjp(lambda layer_in, flat_params: layer(layer_in, flat_params, seq_segs, seq_places), seq_in, weights)
        grad_in, grad_flat = pullback(seq_cot)
        return (running + grad_flat, (output.astype(jnp.bfloat16), grad_in.astype(jnp.bfloat16)))
    running, (outputs, grad_inputs) = lax.scan(one_sequence, jnp.zeros((P_SIZE,), jnp.float32), (inputs, upstream, seg_rows, place_rows))
    param_grad = running * (1.0 / math.sqrt(TOKENS))
    new_first = 0.9 * first_moment + 0.1 * param_grad
    new_second = 0.95 * second_moment + 0.05 * param_grad * param_grad
    corrected_first = new_first / (1.0 - 0.9 ** STEP)
    corrected_second = new_second / (1.0 - 0.95 ** STEP)
    param_update = -0.1 * (corrected_first / (jnp.sqrt(corrected_second) + 1e-08) + 0.01 * params)
    return (outputs.reshape(TOKENS, D), grad_inputs.reshape(TOKENS, D), param_grad, param_update, new_first, new_second)
```

```python
import functools
import math

import jax
import jax.numpy as jnp
from jax import lax
from jax.experimental import pallas as pl
from jax.experimental.pallas import tpu as pltpu
from jax.sharding import PartitionSpec as P

D = 512
HEADS = 8
HEAD = 64
ROT = 16
FF = 2048
STEP = 4
NORM_EPS = 1e-05
ROPE_BASE = 10000.0
INV_ROOT_TWO = 0.7071067811865476
INV_ROOT_TWO_PI = 0.3989422804014327


START = {"qkv": 0, "out": 6144, "up": 8192, "down": 16384, "small": 24576}
WIDTH = {"qkv": 12, "out": 4, "up": 16, "down": 4, "small": 1}
SHARD_UNITS = 6157
PHASES = 4
PIECE = 1600
GROUPS = ((0,), (1,), (2,), (3,))


def up_blocks(phase):
    return [phase, 4 + 3 * phase, 5 + 3 * phase, 6 + 3 * phase]


def piece_parts(shard, phase):
    parts = []
    if shard == 0:
        for i in range(3):
            parts.append((512 * i, "qkv", 4 * i + phase, 0, 512))
        if phase == 0:
            for c in range(4):
                parts.append((1536 + 16 * c, "out", c, 0, 16))
    elif shard == 1:
        for c in range(4):
            parts.append((128 * c, "out", c, 128 * phase, 128))
        for i, c in enumerate(up_blocks(phase)):
            parts.append((512 + 272 * i, "up", c, 0, 272))
    elif shard == 2:
        for i, c in enumerate(up_blocks(phase)):
            parts.append((256 * i, "up", c, 256, 256))
        for c in range(4):
            parts.append((1024 + 128 * c, "down", c, 128 * phase, 128))
        if phase == 0:
            for c in range(4):
                parts.append((1536 + 16 * c, "down", c, 512, 16))
    else:
        for c in range(4):
            parts.append((384 * c, "down", c, 512 + 384 * phase, 384))
    return parts


def split_part(shard, part):
    at, name, block, first, count = part
    low, high = shard * SHARD_UNITS, (shard + 1) * SHARD_UNITS

    def unit(row):
        return START[name] + row * WIDTH[name] + block

    tiles = []
    for t in range(0, count, 16):
        inside = [low <= unit(first + t + r) < high for r in range(min(16, count - t))]
        tiles.append((all(inside), inside))
    runs, t = [], 0
    while t < len(tiles):
        if tiles[t][0]:
            end = t
            while end < len(tiles) and tiles[end][0]:
                end += 1
            rows = min(16 * end, count) - 16 * t
            runs.append((True, at + 16 * t, unit(first + 16 * t) - low, WIDTH[name], rows))
            t = end
        else:
            inside = tiles[t][1]
            rows = [r for r in range(len(inside)) if inside[r]]
            units = [unit(first + 16 * t + r) - low for r in rows]
            runs.append((False, at + 16 * t, units, rows, 16))
            t += 1
    return runs


def small_runs(shard):
    if shard != 3:
        return []
    base = START["small"] - 3 * SHARD_UNITS
    runs = [(True, 1536, base, 1, 48)]
    runs.append((False, 1584, [base + 48 + r for r in range(4)], list(range(4)), 16))
    return runs


def prep_kernel(sid_ref, flat_ref, *outs):
    sid = sid_ref[0]
    for shard in range(4):

        @pl.when(sid == shard)
        def _(shard=shard):
            for phase in range(PHASES):
                group = next(g for g in range(len(GROUPS)) if phase in GROUPS[g])
                out = outs[group].at[GROUPS[group].index(phase)]
                runs = []
                for part in piece_parts(shard, phase):
                    runs.extend(split_part(shard, part))
                if phase == 0:
                    runs.extend(small_runs(shard))
                covered = 0
                for full, at, where, how, rows in runs:
                    covered += rows
                    if full:
                        value = flat_ref[pl.ds(where, rows, stride=how), :]
                        out[pl.ds(at, rows), :] = value.astype(jnp.bfloat16)
                    else:
                        lane_rows = lax.broadcasted_iota(jnp.int32, (16, 128), 0)
                        value = jnp.zeros((16, 128), jnp.float32)
                        for unit, row in zip(where, how):
                            one = jnp.broadcast_to(flat_ref[pl.ds(unit, 1), :], (16, 128))
                            value = jnp.where(lane_rows == row, one, value)
                        out[pl.ds(at, 16), :] = value.astype(jnp.bfloat16)
                if covered < PIECE:
                    out[pl.ds(covered, PIECE - covered), :] = jnp.zeros(
                        (PIECE - covered, 128), jnp.bfloat16
                    )


def prep(sid, flat):
    return pl.pallas_call(
        prep_kernel,
        out_shape=[jax.ShapeDtypeStruct((len(g), PIECE, 128), jnp.bfloat16) for g in GROUPS],
        in_specs=[
            pl.BlockSpec(memory_space=pltpu.SMEM),
            pl.BlockSpec(memory_space=pltpu.VMEM),
        ],
        out_specs=[pl.BlockSpec(memory_space=pltpu.VMEM)] * len(GROUPS),
        compiler_params=pltpu.CompilerParams(vmem_limit_bytes=16 * 1024 * 1024),
        name="prep",
    )(sid, flat)


ADAM_ROWS = 400


def adam_kernel(sid_ref, factor, *refs):
    pieces = refs[:PHASES]
    moment_one, moment_two, weights = refs[PHASES : PHASES + 3]
    out_grad, out_update, out_one, out_two = refs[PHASES + 3 : PHASES + 7]
    flat = refs[PHASES + 7]
    sid = sid_ref[0]
    step = pl.program_id(0)
    for shard in range(4):

        @pl.when((step == 0) & (sid == shard))
        def _(shard=shard):
            for phase in range(PHASES):
                runs = []
                for part in piece_parts(shard, phase):
                    runs.extend(split_part(shard, part))
                if phase == PHASES - 1:
                    runs.extend(small_runs(shard))
                for full, at, where, how, rows in runs:
                    value = pieces[phase][pl.ds(at, rows), :].astype(jnp.float32)
                    if full:
                        flat[pl.ds(where, rows, stride=how), :] = value
                    else:
                        for unit, row in zip(where, how):
                            flat[pl.ds(unit, 1), :] = value[row : row + 1, :]

    grad = flat[pl.ds(pl.multiple_of(step * ADAM_ROWS, 8), ADAM_ROWS), :] * factor
    new_one = 0.9 * moment_one[...] + 0.1 * grad
    new_two = 0.95 * moment_two[...] + 0.05 * grad * grad
    corrected_one = new_one / (1.0 - 0.9**STEP)
    corrected_two = new_two / (1.0 - 0.95**STEP)
    out_grad[...] = grad
    out_one[...] = new_one
    out_two[...] = new_two
    out_update[...] = -0.1 * (
        corrected_one / (jnp.sqrt(corrected_two) + 1e-08) + 0.01 * weights[...]
    )


def adam(sid, pieces, moment_one, moment_two, weights, factor):
    steps = -(-SHARD_UNITS // ADAM_ROWS)
    block = pl.BlockSpec((ADAM_ROWS, 128), lambda i: (i, 0))
    whole = pl.BlockSpec((PIECE, 128), lambda i: (0, 0))

    def kernel(sid_ref, *refs):
        adam_kernel(sid_ref, factor, *refs)

    return pl.pallas_call(
        kernel,
        grid=(steps,),
        out_shape=[jax.ShapeDtypeStruct((SHARD_UNITS, 128), jnp.float32)] * 4,
        in_specs=[pl.BlockSpec(memory_space=pltpu.SMEM)] + [whole] * PHASES + [block] * 3,
        out_specs=[block] * 4,
        scratch_shapes=[pltpu.VMEM((steps * ADAM_ROWS, 128), jnp.float32)],
        compiler_params=pltpu.CompilerParams(vmem_limit_bytes=24 * 1024 * 1024),
        name="adam",
    )(sid, *pieces, moment_one, moment_two, weights)


CORE = [(i, i ^ 1) for i in range(4)]
CROSS = [(i, i ^ 2) for i in range(4)]


def swap_core(v):
    return lax.ppermute(v, "shard", CORE)


def swap_cross(v):
    return lax.ppermute(v, "shard", CROSS)


def swap_rep(v, bit):
    return lax.ppermute(v, "rep", [(i, i ^ bit) for i in range(lax.axis_size("rep"))])


def nn(a, b):
    return lax.dot_general(a, b, (((1,), (0,)), ((), ())), preferred_element_type=jnp.float32)


def nt(a, b):
    return lax.dot_general(a, b, (((1,), (1,)), ((), ())), preferred_element_type=jnp.float32)


def tn(a, b):
    return lax.dot_general(a, b, (((0,), (0,)), ((), ())), preferred_element_type=jnp.float32)


def small_row(small, first, count):
    rows = [small[pl.ds(first + i, 1), :] for i in range(count)]
    return jnp.concatenate(rows, axis=1).astype(jnp.float32)


def put_row(small, first, row, add=False):
    for i in range(row.shape[1] // 128):
        part = row[:, 128 * i : 128 * i + 128]
        if add:
            part = part + small[pl.ds(first + i, 1), :]
        small[pl.ds(first + i, 1), :] = part


def column_sum(v):
    return jnp.sum(v, axis=0, keepdims=True)


SEQ = 512


def start_phase(tokens, cotangent, small, normed, x_one, x_one_t, x_two, x_two_t, sums):
    inputs = tokens[...].astype(jnp.float32)
    center = inputs - jnp.mean(inputs, axis=1, keepdims=True)
    inv_std = lax.rsqrt(jnp.mean(center * center, axis=1, keepdims=True) + NORM_EPS)
    unit = center * inv_std
    normed[...] = unit
    one = (unit * small_row(small, 36, 4) + small_row(small, 40, 4)).astype(jnp.bfloat16)
    x_one[...] = one
    x_one_t[...] = one.T
    two = (unit * small_row(small, 44, 4) + small_row(small, 48, 4)).astype(jnp.bfloat16)
    x_two[...] = two
    x_two_t[...] = two.T
    sums[...] = jnp.zeros((64, 128), jnp.float32)
    total = column_sum(cotangent[...].astype(jnp.float32))
    put_row(sums, 12, total)
    put_row(sums, 32, total)


def attention_phase(phase, w, g, r):
    lane = lax.broadcasted_iota(jnp.int32, (SEQ, 128), 1)
    first_head = lane < HEAD
    w_qkv = jnp.concatenate([w[0, pl.ds(512 * i, 512), :] for i in range(3)], axis=1)
    bias = jnp.concatenate([small_row(r.small, 4 * i + phase, 1) for i in range(3)], axis=1)
    projected = nn(r.x_one[...], w_qkv) + bias

    def turn(v, sign):
        return (
            v * r.cosine[...]
            + sign * (pltpu.roll(v, 120, 1) * r.sine_a[...] + pltpu.roll(v, 8, 1) * r.sine_b[...])
        )

    query = (turn(projected[:, :128], 1.0) * HEAD**-0.5).astype(jnp.bfloat16)
    key = turn(projected[:, 128:256], 1.0).astype(jnp.bfloat16)
    value = projected[:, 256:].astype(jnp.bfloat16)
    key_t = key.T
    value_t = value.T
    w_out = jnp.concatenate([w[1, pl.ds(128 * c, 128), :] for c in range(4)], axis=1)
    grad_merged = nt(r.cotangent[...], w_out).astype(jnp.bfloat16)
    zero = jnp.zeros((SEQ, 128), jnp.bfloat16)
    grad_value = [jnp.zeros((256, 128), jnp.float32) for _ in range(2)]
    grad_key = [jnp.zeros((256, 128), jnp.float32) for _ in range(2)]
    merged_t, query_t = [], []
    for h in range(2):
        mine = first_head if h == 0 else jnp.logical_not(first_head)
        key_h = jnp.where(mine, key, zero)
        value_h = jnp.where(mine, value, zero)
        query_h = jnp.where(mine, query, zero)
        grad_h = jnp.where(mine, grad_merged, zero)
        outs, grads = [], []
        for b in range(2):
            seen = 256 * (b + 1)
            cols = slice(256 * b, 256 * b + 256)
            score = nt(key_h[:seen], query[cols]) + r.mask[pl.ds(0, seen), pl.ds(256 * b, 256)]
            peak = jnp.max(score, axis=0, keepdims=True)
            terms = jnp.exp(score - peak)
            probs = terms * (1.0 / jnp.sum(terms, axis=0, keepdims=True))
            low = probs.astype(jnp.bfloat16)
            outs.append(nn(value_t[64 * h : 64 * h + 64, :seen], low))
            grad_probs = nt(value_h[:seen], grad_merged[cols])
            both = grad_probs * probs
            grad_score = (both - probs * column_sum(both)).astype(jnp.bfloat16)
            grads.append(nn(key_t[64 * h : 64 * h + 64, :seen], grad_score))
            more_value = nn(low, grad_h[cols])
            more_key = nn(grad_score, query_h[cols])
            for i in range(b + 1):
                grad_value[i] = grad_value[i] + more_value[256 * i : 256 * i + 256]
                grad_key[i] = grad_key[i] + more_key[256 * i : 256 * i + 256]
        merged_t.append(jnp.concatenate(outs, axis=1))
        query_t.append(jnp.concatenate(grads, axis=1))
    merged_t = jnp.concatenate(merged_t, axis=0).astype(jnp.bfloat16)
    grad_query = (jnp.concatenate(query_t, axis=0) * HEAD**-0.5).T
    grad_proj = jnp.concatenate(
        [
            turn(grad_query, -1.0),
            turn(jnp.concatenate(grad_key, axis=0), -1.0),
            jnp.concatenate(grad_value, axis=0),
        ],
        axis=1,
    ).astype(jnp.bfloat16)
    grad_w = nn(r.x_one_t[...], grad_proj).astype(jnp.bfloat16)
    total = column_sum(grad_proj.astype(jnp.float32))
    for i in range(3):
        g[0, pl.ds(512 * i, 512), :] = grad_w[:, 128 * i : 128 * i + 128]
        put_row(r.sums, 4 * i + phase, total[:, 128 * i : 128 * i + 128])
    grad_in = nt(grad_proj, w_qkv)
    put_row(r.sums, 40, column_sum(grad_in), add=True)
    put_row(r.sums, 36, column_sum(grad_in * r.normed[...]), add=True)
    r.add_grad(grad_in * small_row(r.small, 36, 4))
    r.add_out(tn(merged_t, w_out))
    grad_out = nn(merged_t, r.cotangent[...]).astype(jnp.bfloat16)
    for c in range(4):
        g[1, pl.ds(128 * c, 128), :] = grad_out[:, 128 * c : 128 * c + 128]
        if phase == 0:
            g[0, pl.ds(1536 + 16 * c, 16), :] = grad_out[:16, 128 * c : 128 * c + 128]


def feed_forward_phase(phase, w, g, r):
    w_up = jnp.concatenate(
        [
            jnp.concatenate(
                [w[1, pl.ds(512 + 272 * i, 256), :], w[2, pl.ds(256 * i, 256), :]], axis=0
            )
            for i in range(4)
        ],
        axis=1,
    )
    w_down = jnp.concatenate(
        [
            jnp.concatenate([w[2, pl.ds(1024 + 128 * c, 128), :] for c in range(4)], axis=1),
            jnp.concatenate([w[3, pl.ds(384 * c, 384), :] for c in range(4)], axis=1),
        ],
        axis=0,
    )
    bias = jnp.concatenate([small_row(r.small, 16 + c, 1) for c in up_blocks(phase)], axis=1)
    hidden = nn(r.x_two[...], w_up) + bias
    grad_act = nt(r.cotangent[...], w_down)
    gate = 0.5 + 0.5 * lax.erf(hidden * INV_ROOT_TWO)
    active = (hidden * gate).astype(jnp.bfloat16)
    slope = gate + hidden * jnp.exp(-0.5 * hidden * hidden) * INV_ROOT_TWO_PI
    grad_hidden = (grad_act * slope).astype(jnp.bfloat16)
    r.add_out(nn(active, w_down))
    grad_up = nn(r.x_two_t[...], grad_hidden).astype(jnp.bfloat16)
    total = column_sum(grad_hidden.astype(jnp.float32))
    for i, c in enumerate(up_blocks(phase)):
        side = grad_up[:, 128 * i : 128 * i + 128]
        g[1, pl.ds(512 + 272 * i, 272), :] = side[:272]
        g[2, pl.ds(256 * i, 256), :] = side[256:]
        put_row(r.sums, 16 + c, total[:, 128 * i : 128 * i + 128])
    grad_down = tn(active, r.cotangent[...]).astype(jnp.bfloat16)
    for c in range(4):
        side = grad_down[:, 128 * c : 128 * c + 128]
        g[2, pl.ds(1024 + 128 * c, 128), :] = side[:128]
        g[3, pl.ds(384 * c, 384), :] = side[128:]
        if phase == 0:
            g[2, pl.ds(1536 + 16 * c, 16), :] = side[128:144]
    grad_in = nt(grad_hidden, w_up)
    put_row(r.sums, 48, column_sum(grad_in), add=True)
    put_row(r.sums, 44, column_sum(grad_in * r.normed[...]), add=True)
    r.add_grad(grad_in * small_row(r.small, 44, 4))


class Refs:
    pass


STATE = ("normed", "x_one", "x_one_t", "x_two", "x_two_t", "small", "sums", "out", "grad")
TABLES = ("tokens", "cotangent", "cosine", "sine_a", "sine_b", "mask")
CONSTANT = STATE[:6]


def group_kernel(group, *refs):
    phases = GROUPS[group]
    first = group == 0
    last = group == len(GROUPS) - 1
    refs = list(refs)
    r = Refs()
    parts = [refs.pop(0) for _ in range(4)]
    for name in TABLES:
        setattr(r, name, refs.pop(0))
    before = {}
    if not first:
        for name in STATE:
            before[name] = refs.pop(0)
    kept, sent = refs.pop(0), refs.pop(0)
    after = {}
    for name in STATE if first else STATE[6:]:
        after[name] = refs.pop(0)
    w_all, g_all, in_sems, out_sems = refs
    sid = lax.axis_index("shard").astype(jnp.int32)
    loads = []
    for k in range(4):
        for i in range(len(phases)):
            loads.append(
                pltpu.make_async_copy(
                    parts[k].at[i], w_all.at[i, lax.bitwise_xor(sid, k)], in_sems.at[k, i]
                )
            )
    for copy in loads:
        copy.start()
    for copy in loads:
        copy.wait()
    for name in STATE:
        setattr(r, name, after[name] if first or name in STATE[6:] else before[name])
    if first:
        r.small[...] = w_all[0, 3, pl.ds(1536, 64), :]
        start_phase(
            r.tokens, r.cotangent, r.small, r.normed, r.x_one, r.x_one_t, r.x_two, r.x_two_t, r.sums
        )
    else:
        r.sums[...] = before["sums"][...]
    fresh = {"out": True, "grad": True}

    def adder(name):
        def add(v):
            ref = getattr(r, name)
            if fresh[name]:
                ref[...] = v if first else before[name][...] + v
                fresh[name] = False
            else:
                ref[...] = ref[...] + v

        return add

    r.add_out, r.add_grad = adder("out"), adder("grad")
    for i, phase in enumerate(phases):
        w, g = w_all.at[i], g_all.at[i]
        for c in range(4):
            if phase == 0:
                edge = pl.ds(1536 + 16 * c, 16)
                rows = pl.ds(128 * c, 16)
                w[1, rows, :] = w[1, rows, :] + w[0, edge, :]
                rows = pl.ds(384 * c, 16)
                w[3, rows, :] = w[3, rows, :] + w[2, edge, :]
            rows = pl.ds(256 * c, 16)
            w[2, rows, :] = w[2, rows, :] + w[1, pl.ds(768 + 272 * c, 16), :]
        attention_phase(phase, w, g, r)
        feed_forward_phase(phase, w, g, r)
        rest = jnp.zeros((64, 128), jnp.bfloat16)
        if phase != 0:
            g[0, pl.ds(1536, 64), :] = rest
            g[2, pl.ds(1536, 64), :] = rest
        if phase == PHASES - 1:
            rest = r.sums[...].astype(jnp.bfloat16)
        g[3, pl.ds(1536, 64), :] = rest
    stores = []
    for k in range(4):
        to = kept if k % 2 == 0 else sent
        for i in range(len(phases)):
            stores.append(
                pltpu.make_async_copy(
                    g_all.at[i, lax.bitwise_xor(sid, k)], to.at[k // 2, i], out_sems.at[k, i]
                )
            )
    for copy in stores:
        copy.start()
    for copy in stores:
        copy.wait()


def run_group(group, parts, tables, state):
    count = len(GROUPS[group])
    first = group == 0
    f32, bf16 = jnp.float32, jnp.bfloat16
    kinds = {
        "normed": ((SEQ, D), f32),
        "x_one": ((SEQ, D), bf16),
        "x_one_t": ((D, SEQ), bf16),
        "x_two": ((SEQ, D), bf16),
        "x_two_t": ((D, SEQ), bf16),
        "small": ((64, 128), bf16),
        "sums": ((64, 128), f32),
        "out": ((SEQ, D), f32),
        "grad": ((SEQ, D), f32),
    }
    hbm = pl.BlockSpec(memory_space=pl.ANY)
    vmem = pl.BlockSpec(memory_space=pltpu.VMEM)
    names = STATE if first else STATE[6:]
    operands = list(parts) + [tables[n] for n in TABLES]
    if not first:
        operands += [state[n] for n in STATE]
    halves = jax.ShapeDtypeStruct((2, count, PIECE, 128), bf16)
    results = pl.pallas_call(
        functools.partial(group_kernel, group),
        out_shape=[halves, halves] + [jax.ShapeDtypeStruct(*kinds[n]) for n in names],
        in_specs=[hbm] * 4 + [vmem] * (len(operands) - 4),
        out_specs=[hbm] * 2 + [vmem] * len(names),
        scratch_shapes=[
            pltpu.VMEM((count, 4, PIECE, 128), bf16),
            pltpu.VMEM((count, 4, PIECE, 128), bf16),
            pltpu.SemaphoreType.DMA((4, count)),
            pltpu.SemaphoreType.DMA((4, count)),
        ],
        compiler_params=pltpu.CompilerParams(vmem_limit_bytes=36 * 1024 * 1024),
        cost_estimate=pl.CostEstimate(
            flops=count * 4_000_000_000, bytes_accessed=8_000_000, transcendentals=count * 2_000_000
        ),
        name=f"group_{group}",
    )(*operands)
    new_state = dict(state)
    for name, value in zip(names, results[2:]):
        new_state[name] = value
    return results[0], results[1], new_state


def final_kernel(tokens, cotangent, normed, out, grad, small, mixed, input_grad):
    inputs = tokens[...].astype(jnp.float32)
    bias = small_row(small, 12, 4) + small_row(small, 32, 4)
    mixed[...] = (inputs + out[...] + bias).astype(jnp.bfloat16)
    center = inputs - jnp.mean(inputs, axis=1, keepdims=True)
    inv_std = lax.rsqrt(jnp.mean(center * center, axis=1, keepdims=True) + NORM_EPS)
    unit = normed[...]
    grads = grad[...]
    change = inv_std * (
        grads
        - jnp.mean(grads, axis=1, keepdims=True)
        - unit * jnp.mean(grads * unit, axis=1, keepdims=True)
    )
    input_grad[...] = (cotangent[...].astype(jnp.float32) + change).astype(jnp.bfloat16)


def finish(tokens, cotangent, state):
    vmem = pl.BlockSpec(memory_space=pltpu.VMEM)
    return pl.pallas_call(
        final_kernel,
        out_shape=[jax.ShapeDtypeStruct((SEQ, D), jnp.bfloat16)] * 2,
        in_specs=[vmem] * 6,
        out_specs=[vmem] * 2,
        compiler_params=pltpu.CompilerParams(vmem_limit_bytes=24 * 1024 * 1024),
        name="finish",
    )(tokens, cotangent, state["normed"], state["out"], state["grad"], state["small"])


def make_tables(tokens, cotangent, positions):
    half = ROT // 2
    frequency = ROPE_BASE ** (-jnp.arange(half, dtype=jnp.float32) * 2.0 / ROT)
    angles = positions.astype(jnp.float32)[:, None] * frequency[None, :]
    cosine, sine = jnp.cos(angles), jnp.sin(angles)
    rest = (SEQ, HEAD - ROT)
    none = jnp.zeros((SEQ, half), jnp.float32)

    def spread(a, b, fill):
        one = jnp.concatenate([a, b, jnp.full(rest, fill, jnp.float32)], axis=1)
        return jnp.concatenate([one, one], axis=1)

    index = jnp.arange(SEQ, dtype=jnp.int32)
    seen = (index[:, None] <= index[None, :]) & (index[:, None] >= (index - positions)[None, :])
    return {
        "tokens": tokens,
        "cotangent": cotangent,
        "cosine": spread(cosine, cosine, 1.0),
        "sine_a": spread(-sine, none, 0.0),
        "sine_b": spread(none, sine, 0.0),
        "mask": jnp.where(seen, 0.0, -1e30).astype(jnp.float32),
    }


def add_up(kept, sent, reps):
    got = swap_core(sent)
    f32, bf16 = jnp.float32, jnp.bfloat16
    across = swap_cross((kept[1].astype(f32) + got[1].astype(f32)).astype(bf16))
    total = kept[0].astype(f32) + got[0].astype(f32) + across.astype(f32)
    count = total.shape[0]
    rows = total.reshape(2, count * PIECE // 2, 128)
    bit = lax.bitwise_and(lax.axis_index("rep"), 1)
    mine = lax.dynamic_index_in_dim(rows, bit, 0, False)
    other = lax.dynamic_index_in_dim(rows, 1 - bit, 0, False).astype(bf16)
    mine = mine + swap_rep(other, 1).astype(f32)
    step = 2
    while step < reps:
        sent = mine.astype(bf16)
        mine = sent.astype(f32) + swap_rep(sent, step).astype(f32)
        step = 2 * step
    mine = mine.astype(bf16)
    other = swap_rep(mine, 1)
    first = jnp.where(bit == 0, mine, other)
    second = jnp.where(bit == 0, other, mine)
    return jnp.concatenate([first, second]).reshape(count, PIECE, 128)


def local(tokens, cotangent, segments, positions, params, first_moment, second_moment):
    sid = lax.axis_index("shard").astype(jnp.int32).reshape(1)
    flat = params.reshape(SHARD_UNITS, 128)
    reps = lax.axis_size("rep")
    tables = make_tables(tokens, cotangent, positions)
    owned = prep(sid, flat)
    state = {}
    reduced = []
    for group in range(len(GROUPS)):
        mate = swap_core(owned[group])
        cross = swap_cross(owned[group])
        both = swap_core(cross)
        kept, sent, state = run_group(group, (owned[group], mate, cross, both), tables, state)
        reduced.append(add_up(kept, sent, reps))
    mixed, input_grad = finish(tokens, cotangent, state)
    pieces = [reduced[g][i] for g in range(len(GROUPS)) for i in range(len(GROUPS[g]))]
    factor = 1.0 / math.sqrt(tokens.shape[0] * lax.axis_size("shard") * reps)
    results = adam(
        sid,
        pieces,
        first_moment.reshape(SHARD_UNITS, 128),
        second_moment.reshape(SHARD_UNITS, 128),
        flat,
        factor,
    )
    return (mixed, input_grad, *[v.reshape(-1) for v in results])


def solution(mesh):
    in_specs = (
        P(("shard", "rep"), None),
        P(("shard", "rep"), None),
        P(("shard", "rep")),
        P(("shard", "rep")),
        P("shard"),
        P("shard"),
        P("shard"),
    )
    out_specs = (
        P(("shard", "rep"), None),
        P(("shard", "rep"), None),
        P("shard"),
        P("shard"),
        P("shard"),
        P("shard"),
    )
    return jax.shard_map(local, mesh=mesh, in_specs=in_specs, out_specs=out_specs, check_vma=False)
```
